32 devices in a mesh: dp: 4 (over z), vocab: 8 (over y, x, core).
Axes of the slice: x: 2, y: 2, z: 4, core: 2. Of those that a mesh axis runs over, the one named last changes fastest.
Arguments:
- query_hidden: bfloat16 [128, 4096], P('dp', 'vocab'), may hold values from -6 to 6
- passage_hidden_rows: bfloat16 [384, 4096], P('dp', 'vocab'), may hold values from -6 to 6
- head_weight: bfloat16 [4096, 128256], P(None, ('dp', 'vocab')), may hold values from -0.09375 to 0.09375
- head_bias: bfloat16 [128256], P(('dp', 'vocab')), may hold values from -4 to 4
- query_mask: int32 [8, 16], P('dp'), may hold values from 0 to 1, as said below
- passage_mask: int32 [8, 48], P('dp'), may hold values from 0 to 1, as said below
- positives: int32 [8], P('dp'), may hold values from 0 to 7, as said below
Outputs:
- loss: float32 [], replicated
- query_grad: bfloat16 [128, 4096], P('dp', 'vocab')
- passage_grad: bfloat16 [384, 4096], P('dp', 'vocab')
The draws below stay inside these ranges and needn't reach their ends.
Inputs may be any that keep to these rules, and one draw needn't show every extreme that they name: `query_mask`: each row holds 4 or more ones from its first token on, then zeros. `passage_mask`: each row holds 12 or more ones from its first token on, then zeros. `positives`: query i's positive is a passage of its own group: it lies in [(i // 2) * 2, (i // 2 + 1) * 2).
All inputs are finite; a program needn't handle non-finite values.
Results may differ from the reference program's by a relative error of at most 0.013.
Values may be sent and summed in bfloat16 or wider, within the bound.
A program may use at most 128 MiB of HBM per device.

```python
import jax
import jax.numpy as jnp
from jax import lax

D = 4096
VOCAB = 128256
LQ = 16
LP = 48
QUERY_GROUP_SIZE = 2
PAS_GRP = 2
QUERIES = 8
PASSAGES = 8


def prefix_mask(key, text_series, span_extent):
    kept_tokens = jax.random.randint(key, (text_series, 1), max(span_extent // 4, 1), span_extent + 1)
    return (jnp.arange(span_extent, dtype=jnp.int32)[None, :] < kept_tokens).astype(jnp.int32)


def draw_query_mask(key, part):
    return prefix_mask(jax.random.fold_in(key, 11), QUERIES, LQ)


def draw_passage_mask(key, part):
    return prefix_mask(jax.random.fold_in(key, 13), PASSAGES, LP)


def draw_positives(key, part):
    offsets = jax.random.randint(jax.random.fold_in(key, 17), (QUERIES,), 0, PAS_GRP)
    return jnp.arange(QUERIES, dtype=jnp.int32) // QUERY_GROUP_SIZE * PAS_GRP + offsets


def shard_levels(own_key, extent, cuts, low, top_value):
    loudness = 1.0
    for axis_at, blocks in cuts:
        steps = jax.random.uniform(jax.random.fold_in(jax.random.fold_in(own_key, 6), axis_at), (blocks,), jnp.float32, low / len(cuts), top_value / len(cuts))
        loudness = loudness * jnp.repeat(jnp.exp(steps), extent[axis_at] // blocks).reshape((-1,) + (1,) * (len(extent) - 1 - axis_at))
    return loudness


def scatter_about(key, dims, scale, limit, split=(), held_as=jnp.bfloat16):
    entries = scale * jax.random.normal(key, dims, jnp.float32)
    if split:
        entries = entries * shard_levels(key, dims, split, -0.22, 0.18)
    return jnp.clip(entries, -limit, limit).astype(held_as)


def setup_inputs(seed: int = 0) -> dict:
    splits = jax.random.split(jax.random.key(seed), 8)
    query_hidden = scatter_about(splits[0], (QUERIES * LQ, D), 1.0, 6.0, ((0, 4), (1, 8)))
    passage_hidden_rows = scatter_about(splits[1], (PASSAGES * LP, D), 1.0, 6.0, ((0, 4), (1, 8)))
    head_weight = scatter_about(splits[2], (D, VOCAB), D ** -0.5, 0.09375, ((1, 32),))
    head_bias = scatter_about(splits[3], (VOCAB,), 1.0, 4.0, ((0, 32),))
    query_mask = draw_query_mask(jax.random.fold_in(splits[7], 71), 0)
    passage_mask = draw_passage_mask(jax.random.fold_in(splits[7], 71), 0)
    positives = draw_positives(jax.random.fold_in(splits[7], 71), 0)
    return {"query_hidden": query_hidden, "passage_hidden_rows": passage_hidden_rows, "head_weight": head_weight, "head_bias": head_bias, "query_mask": query_mask, "passage_mask": passage_mask, "positives": positives}


logit_divisor = 50.0
loss_scale = 1048576.0
epsilon = 1e-06

def pool_tokens(raw_scores_matrix, token_mask):
    text_series, span_extent = token_mask.shape
    lexical_response = jnp.log1p(jax.nn.softplus(raw_scores_matrix)).reshape(text_series, span_extent, -1)
    retained_flag = token_mask.astype(jnp.float32)
    term_importance = retained_flag[:, :, None] * jnp.exp(lexical_response)
    weight_sum = lax.optimization_barrier(jnp.sum(term_importance, axis=1))
    term_total_count = lax.optimization_barrier(jnp.sum(retained_flag, axis=1))[:, None]
    return (jnp.log(weight_sum / term_total_count), term_importance, weight_sum)

def spread(rep_grad, term_importance, weight_sum, raw_scores_matrix):
    text_series, span_extent, columns = term_importance.shape
    token_share = term_importance / weight_sum[:, None, :] * rep_grad[:, None, :]
    act_slope = jax.nn.sigmoid(raw_scores_matrix) / (1.0 + jax.nn.softplus(raw_scores_matrix))
    return token_share.reshape(text_series * span_extent, columns) * act_slope

def contrast(dots, query_sq, passage_sq, targets):
    question_length_measure = jnp.sqrt(query_sq + epsilon)
    document_length_measure = jnp.sqrt(passage_sq + epsilon)
    multiplier_coefficient = logit_divisor / (question_length_measure[:, None] * document_length_measure[None, :])
    scores = dots * multiplier_coefficient
    exp_scores = jnp.exp(scores)
    exp_total = lax.optimization_barrier(jnp.sum(exp_scores, axis=1))
    onehot = (targets[:, None] == jnp.arange(dots.shape[1], dtype=jnp.int32)[None, :]).astype(jnp.float32)
    loss = jnp.mean(jnp.log(exp_total) - lax.optimization_barrier(jnp.sum(onehot * scores, axis=1)))
    score_grad = (exp_scores / exp_total[:, None] - onehot) * (loss_scale / dots.shape[0])
    dots_grad = score_grad * multiplier_coefficient
    score_back = score_grad * scores
    query_coef = -lax.optimization_barrier(jnp.sum(score_back, axis=1)) / (query_sq + epsilon)
    passage_coef = -lax.optimization_barrier(jnp.sum(score_back, axis=0)) / (passage_sq + epsilon)
    return (loss, dots_grad, query_coef, passage_coef)

def reference(query_hidden, passage_hidden_rows, head_weight, head_bias, query_mask, passage_mask, positives):
    blocks = 8
    vocab_cols = VOCAB // blocks

    def weight_at(block_index):
        offset = (block_index * vocab_cols).astype(jnp.int32)
        weight_block = lax.dynamic_slice_in_dim(head_weight, offset, vocab_cols, 1)
        bias_block = lax.dynamic_slice_in_dim(head_bias, offset, vocab_cols, 0).astype(jnp.float32)
        return (weight_block, bias_block)

    def forward(block_index):
        weight_block, bias_block = weight_at(block_index)
        query_logits = jnp.dot(query_hidden, weight_block, preferred_element_type=jnp.float32) + bias_block
        passage_logits = jnp.dot(passage_hidden_rows, weight_block, preferred_element_type=jnp.float32) + bias_block
        query_rep = pool_tokens(query_logits, query_mask)[0]
        passage_rep = pool_tokens(passage_logits, passage_mask)[0]
        dots = jnp.einsum('qv,pv->qp', query_rep, passage_rep, precision=lax.Precision.HIGHEST)
        return (dots, lax.optimization_barrier(jnp.sum(query_rep * query_rep, axis=1)), lax.optimization_barrier(jnp.sum(passage_rep * passage_rep, axis=1)), query_logits, passage_logits)
    block_dots, block_qsq, block_psq, query_logits, passage_logits = lax.map(forward, jnp.arange(blocks, dtype=jnp.int32))
    loss, dots_grad, query_coef, passage_coef = contrast(lax.optimization_barrier(jnp.sum(block_dots, axis=0)), lax.optimization_barrier(jnp.sum(block_qsq, axis=0)), lax.optimization_barrier(jnp.sum(block_psq, axis=0)), positives)

    def backward(grad_sums, inputs):
        block_index, query_block_rows, passage_block = inputs
        weight_block, bias_block = weight_at(block_index)
        query_rep, query_weight, query_total = pool_tokens(query_block_rows, query_mask)
        passage_rep, passage_weight, passage_total = pool_tokens(passage_block, passage_mask)
        query_rep_grad = jnp.einsum('qp,pv->qv', dots_grad, passage_rep, precision=lax.Precision.HIGHEST) + query_coef[:, None] * query_rep
        passage_rep_grad = jnp.einsum('qp,qv->pv', dots_grad, query_rep, precision=lax.Precision.HIGHEST) + passage_coef[:, None] * passage_rep
        query_dlog = spread(query_rep_grad, query_weight, query_total, query_block_rows).astype(jnp.bfloat16)
        passage_dlog = spread(passage_rep_grad, passage_weight, passage_total, passage_block).astype(jnp.bfloat16)
        contract = (((1,), (1,)), ((), ()))
        query_sum = grad_sums[0] + lax.dot_general(query_dlog, weight_block, contract, preferred_element_type=jnp.float32)
        passage_sum = grad_sums[1] + lax.dot_general(passage_dlog, weight_block, contract, preferred_element_type=jnp.float32)
        return ((query_sum, passage_sum), None)
    zero_pair = (jnp.zeros(query_hidden.shape, jnp.float32), jnp.zeros(passage_hidden_rows.shape, jnp.float32))
    grad_pair, unused = lax.scan(backward, zero_pair, (jnp.arange(blocks, dtype=jnp.int32), query_logits, passage_logits))
    return (loss, grad_pair[0].astype(jnp.bfloat16), grad_pair[1].astype(jnp.bfloat16))
```

```python
import functools

import jax
import jax.numpy as jnp
from jax import lax
from jax.experimental import pallas as pl
from jax.experimental.pallas import tpu as pltpu
from jax.sharding import PartitionSpec as P

logit_divisor = 50.0
loss_scale = 1048576.0
epsilon = 1e-06
HIGH = lax.Precision.HIGHEST


def segments(groups, seq_q, len_q, seq_p, len_p):
    rows = seq_q * len_q + seq_p * len_p
    found = []
    for g in range(groups):
        for i in range(seq_q):
            found.append((g * seq_q + i, g * rows + i * len_q, len_q))
        for j in range(seq_p):
            found.append(
                (groups * seq_q + g * seq_p + j, g * rows + seq_q * len_q + j * len_p, len_p)
            )
    return found


def forward_kernel(
    segs, cols, x_ref, w_ref, bias_ref, mask_ref, count_ref, sig_ref, rep_ref, inv_ref, gram_ref,
    xs, sums
):
    step = pl.program_id(0)
    blocks, rows, width = x_ref.shape
    tile = w_ref.shape[1]

    @pl.when(step == 0)
    def _():
        for v in range(blocks):
            xs[:, v * width : (v + 1) * width] = x_ref[v]
        gram_ref[...] = jnp.zeros_like(gram_ref)

    valid = lax.broadcasted_iota(jnp.int32, (1, tile), 1) < cols - step * tile
    logits = jnp.dot(xs[...], w_ref[...], preferred_element_type=jnp.float32)
    logits = logits + bias_ref[...].astype(jnp.float32)
    small = jnp.exp(-jnp.abs(logits))
    grown = 1.0 + small
    soft = jnp.maximum(logits, 0.0) + jnp.log(grown)
    keep = mask_ref[...]
    weight = keep * (1.0 + soft)
    share = keep * (jnp.where(logits >= 0.0, 1.0, small) / grown)
    sig_ref[...] = jnp.where(valid, share, 0.0).astype(sig_ref.dtype)
    for row, first, size in segs:
        sums[row : row + 1, :] = jnp.sum(weight[first : first + size], axis=0, keepdims=True)
    total = jnp.where(valid, sums[...], 1.0)
    rep = jnp.where(valid, jnp.log(total / count_ref[...]), 0.0)
    rep_ref[...] = rep
    inv_ref[...] = 1.0 / total
    gram_ref[...] += lax.dot_general(
        rep, rep, (((1,), (1,)), ((), ())), precision=HIGH, preferred_element_type=jnp.float32
    )


def contrast(gram, targets, queries):
    passages = gram.shape[0] - queries
    dots = gram[:queries, queries:]
    qq, pp = gram[:queries, :queries], gram[queries:, queries:]

    def eye(n):
        return (
            lax.broadcasted_iota(jnp.int32, (n, n), 0) == lax.broadcasted_iota(jnp.int32, (n, n), 1)
        ).astype(jnp.float32)

    q_col = jnp.sum(qq * eye(queries), axis=1, keepdims=True)
    p_row = jnp.sum(pp * eye(passages), axis=0, keepdims=True)
    scaling = logit_divisor / (jnp.sqrt(q_col + epsilon) * jnp.sqrt(p_row + epsilon))
    scores = dots * scaling
    exp_scores = jnp.exp(scores)
    exp_total = jnp.sum(exp_scores, axis=1, keepdims=True)
    onehot = (targets == lax.broadcasted_iota(jnp.int32, (queries, passages), 1)).astype(
        jnp.float32
    )
    losses = jnp.log(exp_total) - jnp.sum(onehot * scores, axis=1, keepdims=True)
    loss = jnp.sum(losses, axis=0, keepdims=True) / queries
    score_grad = (exp_scores / exp_total - onehot) * (loss_scale / queries)
    dots_grad = score_grad * scaling
    back = score_grad * scores
    q_coef = -jnp.sum(back, axis=1, keepdims=True) / (q_col + epsilon)
    p_coef = -jnp.sum(back, axis=0, keepdims=True) / (p_row + epsilon)
    return loss, dots_grad, q_coef, eye(passages) * p_coef


def backward_kernel(
    segs, queries, chunk, gram_ref, target_ref, rep_ref, inv_ref, sig_ref, w_ref, out_ref, loss_ref,
    dlog, scaled
):
    step = pl.program_id(0)
    cols = w_ref.shape[1]

    @pl.when(step == 0)
    def _():
        loss, dots_grad, q_coef, p_diag = contrast(gram_ref[...], target_ref[...], queries)
        loss_ref[...] = loss

        @pl.loop(0, dlog.shape[1] // chunk)
        def _(c):
            at = pl.ds(pl.multiple_of(c * chunk, chunk), chunk)
            rep = rep_ref[:, at]
            rep_q, rep_p = rep[:queries], rep[queries:]
            dot = functools.partial(
                lax.dot_general, precision=HIGH, preferred_element_type=jnp.float32
            )
            grad_q = dot(dots_grad, rep_p, (((1,), (0,)), ((), ()))) + q_coef * rep_q
            grad_p = dot(dots_grad, rep_q, (((0,), (0,)), ((), ()))) + dot(
                p_diag, rep_p, (((1,), (0,)), ((), ()))
            )
            inv = inv_ref[:, at]
            scaled[:queries] = grad_q * inv[:queries]
            scaled[queries:] = grad_p * inv[queries:]
            for row, first, size in segs:
                dlog[first : first + size, at] = (
                    sig_ref[first : first + size, at].astype(jnp.float32) * scaled[row : row + 1]
                ).astype(dlog.dtype)

    out_ref[0] = lax.dot_general(
        dlog[:, :cols], w_ref[...], (((1,), (1,)), ((), ())), preferred_element_type=jnp.float32
    ).astype(out_ref.dtype)


def compute_forward(x, head_weight, head_bias, keep, count, segs):
    blocks, rows, width = x.shape
    depth, cols = head_weight.shape
    tile = min(512, -(-cols // 128) * 128)
    tiles = -(-cols // tile)
    padded = tiles * tile
    block = tile if tile <= cols else cols
    if block != tile:
        tile, padded = cols, cols
    whole = lambda shape: pl.BlockSpec(shape, lambda i: (0,) * len(shape))
    seqs = count.shape[0]
    return pl.pallas_call(
        functools.partial(forward_kernel, segs, cols),
        grid=(tiles,),
        out_shape=(
            jax.ShapeDtypeStruct((rows, padded), jnp.bfloat16),
            jax.ShapeDtypeStruct((seqs, padded), jnp.float32),
            jax.ShapeDtypeStruct((seqs, padded), jnp.float32),
            jax.ShapeDtypeStruct((seqs, seqs), jnp.float32),
        ),
        in_specs=[
            whole(x.shape),
            pl.BlockSpec((depth, tile), lambda i: (0, i)),
            pl.BlockSpec((1, tile), lambda i: (0, i)),
            whole(keep.shape),
            whole(count.shape),
        ],
        out_specs=(
            pl.BlockSpec((rows, tile), lambda i: (0, i)),
            pl.BlockSpec((seqs, tile), lambda i: (0, i)),
            pl.BlockSpec((seqs, tile), lambda i: (0, i)),
            whole((seqs, seqs)),
        ),
        scratch_shapes=[
            pltpu.VMEM((rows, depth), jnp.bfloat16),
            pltpu.VMEM((seqs, tile), jnp.float32),
        ],
        compiler_params=pltpu.CompilerParams(vmem_limit_bytes=56 << 20),
    )(x, head_weight, head_bias.reshape(1, -1), keep, count)


def compute_backward(gram, targets, rep, inv, sig, head_weight, segs, blocks):
    depth, cols = head_weight.shape
    rows, padded = sig.shape
    seqs, queries = rep.shape[0], targets.shape[0]
    width = depth // blocks
    chunk = min(512, padded)
    whole = lambda shape: pl.BlockSpec(shape, lambda i: (0,) * len(shape))
    return pl.pallas_call(
        functools.partial(backward_kernel, segs, queries, chunk),
        grid=(blocks,),
        out_shape=(
            jax.ShapeDtypeStruct((blocks, rows, width), jnp.bfloat16),
            jax.ShapeDtypeStruct((1, 1), jnp.float32),
        ),
        in_specs=[
            whole(gram.shape),
            whole(targets.shape),
            whole(rep.shape),
            whole(inv.shape),
            whole(sig.shape),
            pl.BlockSpec((width, cols), lambda i: (i, 0)),
        ],
        out_specs=(pl.BlockSpec((1, rows, width), lambda i: (i, 0, 0)), whole((1, 1))),
        scratch_shapes=[
            pltpu.VMEM((rows, padded), jnp.bfloat16),
            pltpu.VMEM((seqs, chunk), jnp.float32),
        ],
        compiler_params=pltpu.CompilerParams(vmem_limit_bytes=56 << 20),
    )(gram, targets, rep, inv, sig, head_weight)


MESH = pl.DeviceIdType.MESH


def greet(peers):
    barrier = pltpu.get_barrier_semaphore()
    for peer in peers:
        pl.semaphore_signal(barrier, inc=1, device_id=peer, device_id_type=MESH)
    pl.semaphore_wait(barrier, len(peers))


def send(src, dst, send_sem, recv_sem, peer):
    return pltpu.make_async_remote_copy(
        src_ref=src,
        dst_ref=dst,
        send_sem=send_sem,
        recv_sem=recv_sem,
        device_id=peer,
        device_id_type=MESH,
    )


def places(groups, blocks):
    g, v = lax.axis_index("dp"), lax.axis_index("vocab")
    partner = v + 1 - 2 * lax.rem(v, 2)
    along_dp = [(lax.rem(g + k, groups), v) for k in range(1, groups)]
    along_vocab = [(g, lax.rem(v + 2 * j, blocks)) for j in range(1, blocks // 2)]
    return g, v, partner, along_dp, along_vocab


def gather_kernel(
    groups, blocks, own_ref, small_ref, out_ref, smalls_ref, local_sem, recv, recv_small, send_dp,
    send_small, send_vocab, send_pair
):
    g, v, partner, along_dp, along_vocab = places(groups, blocks)
    greet(along_dp + along_vocab + [(g, partner)])
    half = blocks // 2
    kept = pltpu.make_async_copy(own_ref, out_ref.at[v, g], local_sem.at[0])
    kept_small = pltpu.make_async_copy(small_ref, smalls_ref.at[g], local_sem.at[1])
    kept.start()
    kept_small.start()
    sent = []

    def go(src, vs, gs, sem, peer):
        copy = send(src, out_ref.at[vs, gs], sem, recv.at[vs, gs], peer)
        copy.start()
        sent.append(copy)

    def arrived(vs, gs):
        send(
            own_ref, out_ref.at[vs, gs], send_pair.at[0, 0], recv.at[vs, gs], (g, partner)
        ).wait_recv()

    for k, peer in enumerate(along_dp):
        go(own_ref, v, g, send_dp.at[k], peer)
    for k, peer in enumerate(along_dp):
        copy = send(small_ref, smalls_ref.at[g], send_small.at[k], recv_small.at[g], peer)
        copy.start()
        sent.append(copy)
    for k in range(groups):
        gs = lax.rem(g - k + groups, groups)
        src = own_ref
        if k:
            arrived(v, gs)
            src = out_ref.at[v, gs]
        for j, peer in enumerate(along_vocab):
            go(src, v, gs, send_vocab.at[k, j], peer)
        go(src, v, gs, send_pair.at[k, 0], (g, partner))
    for k in range(groups):
        gs = lax.rem(g - k + groups, groups)
        for j in range(1, half):
            vs = lax.rem(v - 2 * j + blocks, blocks)
            arrived(vs, gs)
            go(out_ref.at[vs, gs], vs, gs, send_pair.at[k, j], (g, partner))
    for k in range(groups):
        gs = lax.rem(g - k + groups, groups)
        for j in range(half):
            arrived(lax.rem(partner - 2 * j + blocks, blocks), gs)
        if k:
            send(
                small_ref, smalls_ref.at[gs], send_small.at[0], recv_small.at[gs], (g, partner)
            ).wait_recv()
    for copy in sent:
        copy.wait_send()
    kept.wait()
    kept_small.wait()


def gather_all(own, small, groups, blocks):
    half, dma = blocks // 2, pltpu.SemaphoreType.DMA
    anywhere = pl.BlockSpec(memory_space=pl.ANY)
    return pl.pallas_call(
        functools.partial(gather_kernel, groups, blocks),
        out_shape=(
            jax.ShapeDtypeStruct((blocks, groups) + own.shape, own.dtype),
            jax.ShapeDtypeStruct((groups,) + small.shape, small.dtype),
        ),
        in_specs=[anywhere, anywhere],
        out_specs=(anywhere, anywhere),
        scratch_shapes=[
            dma((2,)),
            dma((blocks, groups)),
            dma((groups,)),
            dma((max(groups - 1, 1),)),
            dma((max(groups - 1, 1),)),
            dma((groups, max(half - 1, 1))),
            dma((groups, half)),
        ],
        compiler_params=pltpu.CompilerParams(collective_id=0, has_side_effects=True),
    )(own, small)


def total_kernel(groups, blocks, part_ref, out_ref, buf, local_sem, recv_v, send_v, recv_g, send_g):
    g, v = lax.axis_index("dp"), lax.axis_index("vocab")
    along_dp = [(lax.rem(g + k, groups), v) for k in range(1, groups)]
    along_vocab = [(g, lax.rem(v + j, blocks)) for j in range(1, blocks)]
    greet(along_dp + along_vocab)
    kept = pltpu.make_async_copy(part_ref, buf.at[g, v], local_sem.at[0])
    kept.start()
    sent = []
    for j, peer in enumerate(along_vocab):
        copy = send(part_ref, buf.at[g, v], send_v.at[j], recv_v.at[v], peer)
        copy.start()
        sent.append(copy)
    kept.wait()
    for j in range(1, blocks):
        vs = lax.rem(v - j + blocks, blocks)
        send(part_ref, buf.at[g, vs], send_v.at[0], recv_v.at[vs], (g, vs)).wait_recv()
    for k, peer in enumerate(along_dp):
        copy = send(buf.at[g], buf.at[g], send_g.at[k], recv_g.at[g], peer)
        copy.start()
        sent.append(copy)
    for k in range(1, groups):
        gs = lax.rem(g - k + groups, groups)
        send(buf.at[gs], buf.at[gs], send_g.at[0], recv_g.at[gs], (gs, v)).wait_recv()
    total = jnp.zeros(out_ref.shape, jnp.float32)
    for a in range(groups):
        for b in range(blocks):
            total = total + buf[a, b]
    out_ref[...] = total
    for copy in sent:
        copy.wait_send()


def total_all(part, groups, blocks):
    dma = pltpu.SemaphoreType.DMA
    inside = pl.BlockSpec(memory_space=pltpu.VMEM)
    return pl.pallas_call(
        functools.partial(total_kernel, groups, blocks),
        out_shape=jax.ShapeDtypeStruct(part.shape, part.dtype),
        in_specs=[inside],
        out_specs=inside,
        scratch_shapes=[
            pltpu.VMEM((groups, blocks) + part.shape, jnp.float32),
            dma((1,)),
            dma((blocks,)),
            dma((max(blocks - 1, 1),)),
            dma((groups,)),
            dma((max(groups - 1, 1),)),
        ],
        compiler_params=pltpu.CompilerParams(collective_id=1, has_side_effects=True),
    )(part)


def scatter_kernel(
    groups, blocks, rows_q, a_ref, q_ref, p_ref, pair, pooled, peers, turned, last, recv_pair,
    send_pair, recv_vocab, send_vocab, recv_dp, send_dp
):
    g, v, partner, along_dp, along_vocab = places(groups, blocks)
    greet(along_dp + along_vocab + [(g, partner)])
    half = blocks // 2
    rows = a_ref.shape[1] // groups
    sent = []

    def go(src, dst, send_sem, recv_sem, peer):
        copy = send(src, dst, send_sem, recv_sem, peer)
        copy.start()
        sent.append(copy)

    order = list(range(1, half)) + [0]
    for j in order:
        w = lax.rem(partner + 2 * j, blocks)
        go(a_ref.at[w], pair.at[w // 2], send_pair.at[j], recv_pair.at[w // 2], (g, partner))
    for j in order:
        w = lax.rem(v + 2 * j, blocks)
        at = w // 2
        send(
            a_ref.at[w], pair.at[at], send_pair.at[0], recv_pair.at[at], (g, partner)
        ).wait_recv()
        pooled[at] = (
            a_ref[w].astype(jnp.float32) + pair[at].astype(jnp.float32)
        ).astype(pooled.dtype)
        if j:
            go(
                pooled.at[at],
                peers.at[v // 2],
                send_vocab.at[j - 1],
                recv_vocab.at[v // 2],
                along_vocab[j - 1],
            )
    for j in range(1, half):
        at = lax.rem(v - 2 * j + blocks, blocks) // 2
        send(
            pooled.at[at], peers.at[at], send_vocab.at[0], recv_vocab.at[at], (g, partner)
        ).wait_recv()

    def summed(gs):
        part = pl.ds(pl.multiple_of(gs * rows, rows), rows)
        out = pooled[v // 2, part].astype(jnp.float32)
        for j in range(1, half):
            at = lax.rem(v - 2 * j + blocks, blocks) // 2
            out = out + peers[at, part].astype(jnp.float32)
        return out

    for k, peer in enumerate(along_dp):
        turned[k] = summed(peer[0]).astype(turned.dtype)
        go(turned.at[k], last.at[g], send_dp.at[k], recv_dp.at[g], peer)
    out = summed(g)
    for k in range(1, groups):
        gs = lax.rem(g - k + groups, groups)
        send(turned.at[0], last.at[gs], send_dp.at[0], recv_dp.at[gs], (gs, v)).wait_recv()
        out = out + last[gs].astype(jnp.float32)
    q_ref[...] = out[:rows_q].astype(q_ref.dtype)
    p_ref[...] = out[rows_q:].astype(p_ref.dtype)
    for copy in sent:
        copy.wait_send()


def scatter_all(parts, groups, rows_q):
    blocks, tokens, width = parts.shape
    half, rows, dma = blocks // 2, tokens // groups, pltpu.SemaphoreType.DMA
    inside = pl.BlockSpec(memory_space=pltpu.VMEM)
    block = pltpu.VMEM((half, tokens, width), parts.dtype)
    return pl.pallas_call(
        functools.partial(scatter_kernel, groups, blocks, rows_q),
        out_shape=(
            jax.ShapeDtypeStruct((rows_q, width), parts.dtype),
            jax.ShapeDtypeStruct((rows - rows_q, width), parts.dtype),
        ),
        in_specs=[inside],
        out_specs=(inside, inside),
        scratch_shapes=[
            block,
            block,
            block,
            pltpu.VMEM((max(groups - 1, 1), rows, width), parts.dtype),
            pltpu.VMEM((groups, rows, width), parts.dtype),
            dma((half,)),
            dma((half,)),
            dma((half,)),
            dma((max(half - 1, 1),)),
            dma((groups,)),
            dma((max(groups - 1, 1),)),
        ],
        compiler_params=pltpu.CompilerParams(
            collective_id=2, has_side_effects=True, vmem_limit_bytes=48 << 20
        ),
    )(parts)


def shards(
    query_hidden, passage_hidden_rows, head_weight, head_bias, query_mask, passage_mask, positives
):
    groups, blocks = lax.axis_size("dp"), lax.axis_size("vocab")
    seq_q, len_q = query_mask.shape
    seq_p, len_p = passage_mask.shape
    rows_q = seq_q * len_q
    rows, width = rows_q + seq_p * len_p, query_hidden.shape[1]
    segs = segments(groups, seq_q, len_q, seq_p, len_p)

    own = jnp.concatenate((query_hidden, passage_hidden_rows), 0)
    small = jnp.concatenate((query_mask.reshape(-1), passage_mask.reshape(-1), positives))
    lanes = 128
    held = -(-small.shape[0] // (8 * lanes)) * 8 * lanes
    ints = small.shape[0]
    small = jnp.pad(small, (0, held - ints)).reshape(-1, lanes)
    x, small = gather_all(own, small, groups, blocks)
    x = x.reshape(blocks, groups * rows, width)
    small = small.reshape(groups, held)[:, :ints]
    targets = small[:, rows:].reshape(-1, 1)
    keep = small[:, :rows].astype(jnp.float32)
    count = jnp.concatenate(
        (
            jnp.sum(keep[:, :rows_q].reshape(-1, len_q), axis=1),
            jnp.sum(keep[:, rows_q:].reshape(-1, len_p), axis=1),
        )
    )[:, None]
    sig, rep, inv, gram = compute_forward(
        x, head_weight, head_bias, keep.reshape(-1, 1), count, segs
    )
    gram = total_all(gram, groups, blocks)
    grads, loss = compute_backward(gram, targets, rep, inv, sig, head_weight, segs, blocks)
    query_grad, passage_grad = scatter_all(grads, groups, rows_q)
    return (loss[0, 0], query_grad, passage_grad)


def solution(mesh):
    placed = (
        P("dp", "vocab"),
        P("dp", "vocab"),
        P(None, ("dp", "vocab")),
        P(("dp", "vocab")),
        P("dp", None),
        P("dp", None),
        P("dp"),
    )
    return jax.shard_map(
        shards,
        mesh=mesh,
        in_specs=placed,
        out_specs=(P(), P("dp", "vocab"), P("dp", "vocab")),
        check_vma=False,
    )
```
